32 devices in a mesh: row: 8 (over z, core), col: 4 (over y, x).
Axes of the slice: x: 2, y: 2, z: 4, core: 2. Of those that a mesh axis runs over, the one named last changes fastest.
Arguments:
- tokens: bfloat16 [384, 8192], P(None, 'row'), may hold values from -6 to 6
- grad_out: bfloat16 [384, 8192], P(None, 'row'), may hold values from -6 to 6
- gate_weight: bfloat16 [8192, 22016], P('row', 'col'), may hold values from -0.0625 to 0.0625
- up_weight: bfloat16 [8192, 22016], P('row', 'col'), may hold values from -0.0625 to 0.0625
- down_weight: bfloat16 [8192, 22016], P('row', 'col'), may hold values from -0.0390625 to 0.0390625
- gate_left: bfloat16 [8192, 128], P('row', 'col'), may hold values from -0.01953125 to 0.01953125
- up_left: bfloat16 [8192, 128], P('row', 'col'), may hold values from -0.01953125 to 0.01953125
- down_left: bfloat16 [8192, 128], P('row', 'col'), may hold values from -0.01171875 to 0.01171875
- gate_right: bfloat16 [128, 22016], P('row', 'col'), may hold values from -0.5 to 0.5
- up_right: bfloat16 [128, 22016], P('row', 'col'), may hold values from -0.5 to 0.5
- down_right: bfloat16 [128, 22016], P('row', 'col'), may hold values from -0.5 to 0.5
Outputs:
- mixed: bfloat16 [384, 8192], P('col', 'row')
- input_grad: bfloat16 [384, 8192], P('col', 'row')
- gate_grad: bfloat16 [8192, 22016], P('row', 'col')
- up_grad: bfloat16 [8192, 22016], P('row', 'col')
- down_grad: bfloat16 [8192, 22016], P('row', 'col')
The draws below stay inside these ranges and needn't reach their ends.
All inputs are finite; a program needn't handle non-finite values.
Results may differ from the reference program's by a relative error of at most 0.0072.
Values may be sent and summed in bfloat16 or wider, within the bound.
A program may use at most 192 MiB of HBM per device.

```python
import jax
import jax.numpy as jnp
from jax import lax

D = 8192
FF = 22016
R = 128
TOKENS = 384


def block_levels(key, shape, shards, least, high):
    def one(axis_at, shards_of):
        steps = jax.random.uniform(jax.random.fold_in(jax.random.fold_in(key, 6), axis_at), (shards_of,), jnp.float32, least / len(shards), high / len(shards))
        return jnp.repeat(jnp.exp(steps), shape[axis_at] // shards_of).reshape((-1,) + (1,) * (len(shape) - axis_at - 1))

    loudness = one(*shards[0])
    for cut in shards[1:]:
        loudness = loudness * one(*cut)
    return loudness


def bell_draw(own_key, dims, deviation, reach, split=(), dtype=jnp.bfloat16):
    entries = jax.random.normal(own_key, dims, jnp.float32) * deviation
    if len(split) > 0:
        entries = block_levels(own_key, dims, split, -0.22, 0.18) * entries
    return jnp.clip(entries, min=-reach, max=reach).astype(dtype)


def setup_inputs(seed: int = 0) -> dict:
    keys = jax.random.split(jax.random.key(seed), 12)
    tokens = bell_draw(keys[0], (TOKENS, D), 1.0, 6.0, ((1, 8),))
    grad_out = bell_draw(keys[1], (TOKENS, D), 1.0, 6.0, ((1, 8),))
    gate_weight = bell_draw(keys[2], (D, FF), D ** -0.5, 0.0625, ((0, 8), (1, 4)))
    up_weight = bell_draw(keys[3], (D, FF), D ** -0.5, 0.0625, ((0, 8), (1, 4)))
    down_weight = bell_draw(keys[4], (D, FF), FF ** -0.5, 0.0390625, ((0, 8), (1, 4)))
    gate_left = bell_draw(keys[5], (D, R), (D * 11) ** -0.5, 0.01953125, ((0, 8), (1, 4)))
    up_left = bell_draw(keys[6], (D, R), (D * 11) ** -0.5, 0.01953125, ((0, 8), (1, 4)))
    down_left = bell_draw(keys[7], (D, R), (FF * 11) ** -0.5, 0.01171875, ((0, 8), (1, 4)))
    gate_right = bell_draw(keys[8], (R, FF), R ** -0.5, 0.5, ((0, 8), (1, 4)))
    up_right = bell_draw(keys[9], (R, FF), R ** -0.5, 0.5, ((0, 8), (1, 4)))
    down_right = bell_draw(keys[10], (R, FF), R ** -0.5, 0.5, ((0, 8), (1, 4)))
    return {"tokens": tokens, "grad_out": grad_out, "gate_weight": gate_weight, "up_weight": up_weight, "down_weight": down_weight, "gate_left": gate_left, "up_left": up_left, "down_left": down_left, "gate_right": gate_right, "up_right": up_right, "down_right": down_right}


def merge_weight(base, left, right):
    delta = jnp.dot(left, right, preferred_element_type=jnp.float32)
    return (base.astype(jnp.float32) + delta).astype(jnp.bfloat16)


def reference(tokens, grad_out, gate_weight, up_weight, down_weight, gate_left, up_left, down_left, gate_right, up_right, down_right):
    merged_gate = merge_weight(gate_weight, gate_left, gate_right)
    merged_up = merge_weight(up_weight, up_left, up_right)
    merged_down = merge_weight(down_weight, down_left, down_right)
    gate = jnp.dot(tokens, merged_gate, preferred_element_type=jnp.float32)
    up = jnp.dot(tokens, merged_up, preferred_element_type=jnp.float32)
    sigma = jax.nn.sigmoid(gate)
    hidden = (gate * sigma * up).astype(jnp.bfloat16)
    last_dims = (((1,), (1,)), ((), ()))
    first_dims = (((0,), (0,)), ((), ()))
    mixed = lax.dot_general(hidden, merged_down, last_dims, preferred_element_type=jnp.float32).astype(jnp.bfloat16)
    back = jnp.dot(grad_out, merged_down, preferred_element_type=jnp.float32)
    gate_delta = (back * up * sigma * (1.0 + gate * (1.0 - sigma))).astype(jnp.bfloat16)
    up_delta = (back * gate * sigma).astype(jnp.bfloat16)
    input_grad = lax.dot_general(gate_delta, merged_gate, last_dims, preferred_element_type=jnp.float32)
    input_grad = input_grad + lax.dot_general(up_delta, merged_up, last_dims, preferred_element_type=jnp.float32)
    gate_grad = lax.dot_general(tokens, gate_delta, first_dims, preferred_element_type=jnp.float32).astype(jnp.bfloat16)
    up_grad = lax.dot_general(tokens, up_delta, first_dims, preferred_element_type=jnp.float32).astype(jnp.bfloat16)
    down_grad = lax.dot_general(grad_out, hidden, first_dims, preferred_element_type=jnp.float32).astype(jnp.bfloat16)
    return mixed, input_grad.astype(jnp.bfloat16), gate_grad, up_grad, down_grad
```

```python
import functools

import jax
import jax.numpy as jnp
from jax import lax
from jax.experimental import pallas as pl
from jax.experimental.pallas import tpu as pltpu
from jax.sharding import PartitionSpec as P

F32 = jnp.float32
BF16 = jnp.bfloat16
TILE = 512
CHUNKS = 4
NN = (((1,), (0,)), ((), ()))
NT = (((1,), (1,)), ((), ()))


def dot(a, b, dims=NN):
    return lax.dot_general(a, b, dims, preferred_element_type=F32)


def forward_kernel(half, x_ref, g_ref, wg_ref, wu_ref, wd_ref, keep_ref, send_ref):
    for k, (a_ref, w_ref) in enumerate(((x_ref, wg_ref), (x_ref, wu_ref), (g_ref, wd_ref))):
        w = w_ref[...]
        keep_ref[k] = dot(a_ref[:half], w)
        send_ref[k] = dot(a_ref[half:], w).astype(BF16)


def forward(x, g, weights, start, width):
    tokens, depth = x.shape
    half = tokens // 2
    first = start // TILE
    whole = pl.BlockSpec((tokens, depth), lambda i: (0, 0))
    weight = pl.BlockSpec((depth, TILE), lambda i: (0, first + i))
    out = pl.BlockSpec((3, half, TILE), lambda i: (0, 0, i))
    return pl.pallas_call(
        functools.partial(forward_kernel, half),
        grid=(pl.cdiv(width, TILE),),
        in_specs=[whole, whole, weight, weight, weight],
        out_specs=[out, out],
        out_shape=[
            jax.ShapeDtypeStruct((3, half, width), F32),
            jax.ShapeDtypeStruct((3, half, width), BF16),
        ],
        cost_estimate=pl.CostEstimate(
            flops=6 * tokens * depth * width,
            bytes_accessed=6 * depth * width + 18 * half * width,
            transcendentals=0,
        ),
        name="forward",
    )(x, g, *weights)


def backward_kernel(valid, has_prev, *refs):
    mine_ref, theirs_ref, xt_ref, gt_ref, wg_ref, wu_ref, wd_ref, r_ref = refs[:8]
    prev = refs[8 : 8 + 3 * has_prev]
    if has_prev:
        acc_in, low_in = prev[0], prev[1]
        refs = refs[8 + 5 :]
    else:
        refs = refs[8:]
    acc_ref, low_ref, gg_ref, ug_ref, dg_ref = refs
    step = pl.program_id(0)

    @pl.when(step == 0)
    def _():
        if has_prev:
            acc_ref[...] = acc_in[...]
            low_ref[...] = low_in[...]
        else:
            acc_ref[...] = jnp.zeros_like(acc_ref)
            low_ref[...] = jnp.zeros_like(low_ref)

    def masked(v):
        if valid is None:
            return v
        at = lax.broadcasted_iota(jnp.int32, v.shape, 1) + step * TILE
        return jnp.where(at < valid, v, jnp.zeros_like(v))

    def joined(k):
        return masked(jnp.concatenate([mine_ref[k], theirs_ref[k]], axis=0))

    hidden, gate_delta, up_delta = joined(0), joined(1), joined(2)
    dg_ref[...] = dot(gt_ref[...], hidden).astype(BF16)
    gg_ref[...] = dot(xt_ref[...], gate_delta).astype(BF16)
    ug_ref[...] = dot(xt_ref[...], up_delta).astype(BF16)
    acc_ref[0] += dot(hidden, masked(wd_ref[...]), NT)
    acc_ref[1] += dot(gate_delta, masked(wg_ref[...]), NT) + dot(up_delta, masked(wu_ref[...]), NT)
    low_ref[0] += dot(hidden, masked(r_ref[2]), NT)
    low_ref[1] += dot(gate_delta, masked(r_ref[0]), NT)
    low_ref[2] += dot(up_delta, masked(r_ref[1]), NT)


def backward(mine, theirs, xt, gt, weights, rights, start, width, prev):
    depth, tokens = xt.shape
    half = tokens // 2
    total = weights[0].shape[1]
    rank = rights.shape[1]
    first = start // TILE
    whole = pl.BlockSpec((depth, tokens), lambda i: (0, 0))
    part = pl.BlockSpec((3, half, TILE), lambda i: (0, 0, i))
    weight = pl.BlockSpec((depth, TILE), lambda i: (0, first + i))
    right = pl.BlockSpec((3, rank, TILE), lambda i: (0, 0, first + i))
    acc = pl.BlockSpec((2, tokens, depth), lambda i: (0, 0, 0))
    low = pl.BlockSpec((3, tokens, rank), lambda i: (0, 0, 0))
    anywhere = pl.BlockSpec(memory_space=pl.ANY)
    in_specs = [part, part, whole, whole, weight, weight, weight, right]
    operands = [mine, theirs, xt, gt, *weights, rights]
    aliases = {}
    if prev is not None:
        in_specs += [acc, low, anywhere, anywhere, anywhere]
        operands += list(prev)
        aliases = {8 + k: k for k in range(5)}
    grad = jax.ShapeDtypeStruct((depth, total), BF16)
    return pl.pallas_call(
        functools.partial(backward_kernel, width if width % TILE else None, int(prev is not None)),
        grid=(pl.cdiv(width, TILE),),
        in_specs=in_specs,
        out_specs=[acc, low, weight, weight, weight],
        out_shape=[
            jax.ShapeDtypeStruct((2, tokens, depth), F32),
            jax.ShapeDtypeStruct((3, tokens, rank), F32),
            grad,
            grad,
            grad,
        ],
        input_output_aliases=aliases,
        cost_estimate=pl.CostEstimate(
            flops=12 * tokens * depth * width + 6 * tokens * rank * width,
            bytes_accessed=12 * depth * width + 6 * tokens * width,
            transcendentals=0,
        ),
        name="backward",
    )(*operands)


def shards(
    row,
    tokens,
    grad_out,
    gate_weight,
    up_weight,
    down_weight,
    gate_left,
    up_left,
    down_left,
    gate_right,
    up_right,
    down_right,
):
    line = row // 2
    at = lax.axis_index("row")
    core = at % 2
    place = at // 2
    count = tokens.shape[0]
    half = count // 2
    block = half // line
    width = gate_weight.shape[1]
    mates = [(r, r ^ 1) for r in range(row)]

    def swap(v):
        return lax.ppermute(v, "row", mates)

    def hops(places, step):
        return [(2 * z + c, 2 * (z + step) + c) for z in places for c in range(2)]

    def scatter(own):
        def term(k):
            k = jnp.clip(k, 0, line - 1)
            return lax.dynamic_index_in_dim(own, k, 1, keepdims=False)

        up = term(line - 1 + place)
        down = term(1 - line + place)
        for t in range(1, line):
            up = lax.ppermute(up.astype(BF16), "row", hops(range(t), 1)).astype(F32)
            down = lax.ppermute(
                down.astype(BF16), "row", hops(range(line - t, line), -1)
            ).astype(F32)
            if t < line - 1:
                up = up + term(line - t - 1 + place)
                down = down + term(t + 1 - line + place)
        return up + down + term(place)

    def gather(own):
        ups, downs = [own], [own]
        for t in range(1, line):
            ups.append(lax.ppermute(ups[-1], "row", hops(range(t - 1, line - 1), 1)))
            downs.append(lax.ppermute(downs[-1], "row", hops(range(1, line - t + 1), -1)))
        whole = jnp.zeros((own.shape[0], line) + own.shape[1:], own.dtype)
        whole = lax.dynamic_update_index_in_dim(whole, own, place, 1)
        for d in range(1, line):
            piece = jnp.where(place >= d, ups[d], downs[line - d])
            whole = lax.dynamic_update_index_in_dim(whole, piece, (place + line - d) % line, 1)
        return whole

    def ordered(v, axis):
        return jnp.where(core == 0, v, jnp.roll(v, half, axis))

    x = ordered(tokens, 0)
    g = ordered(grad_out, 0)
    weights = (gate_weight, up_weight, down_weight)

    tiles = -(-width // TILE)
    cuts = [min(width, TILE * -(-tiles * k // CHUNKS)) for k in range(CHUNKS + 1)]
    spans = [(a, b - a) for a, b in zip(cuts, cuts[1:])]
    parts = [forward(x, g, weights, a, n) for a, n in spans]

    rights = jnp.stack([gate_right, up_right, down_right])
    mine = gather(rights)
    theirs = swap(mine)
    pair = jnp.stack([mine, theirs], 1)
    rank = row * rights.shape[1]
    rights = pair.reshape(3, rank, width)

    lefts = lax.all_gather(
        jnp.concatenate([gate_left, up_left, down_left], 0), "col", axis=1, tiled=True
    )
    lefts = lefts.reshape(3, -1, line, 2, rank // row)
    lefts = jnp.where(core == 0, lefts, jnp.flip(lefts, 3))
    lefts = jnp.swapaxes(lefts, 2, 3).reshape(3, -1, rank)
    natural = [dot(x, lefts[0]), dot(x, lefts[1]), dot(g, lefts[2])]
    low = jnp.stack(natural)
    return finish(
        row, core, half, block, line, low, lefts, rights, parts, spans, x, g, weights,
        swap, scatter, gather, ordered,
    )


def finish(
    row, core, half, block, line, low, lefts, rights, parts, spans, x, g, weights,
    swap, scatter, gather, ordered,
):
    rank = low.shape[2]

    def own_ranks(v):
        v = v.reshape(v.shape[:-1] + (2, rank // 2))
        return jnp.where(core == 0, v, jnp.flip(v, -2)).reshape(v.shape[:-2] + (rank,))

    low = own_ranks(low)
    kept = low[:, :half] + swap(low[:, half:])
    low_rows = own_ranks(scatter(kept.reshape(3, line, block, rank)))
    low_rows = low_rows.astype(BF16)

    xt, gt = x.T, g.T
    state = None
    for (start, size), (keep, send) in zip(spans, parts):
        own = keep + swap(send).astype(F32)
        sums = scatter(own.reshape(3, line, block, size))
        cut = rights[:, :, start : start + size]
        gate, up, back = (sums[k] + dot(low_rows[k], cut[k]) for k in range(3))
        sigma = jax.nn.sigmoid(gate)
        hidden = (gate * sigma * up).astype(BF16)
        gate_delta = (back * up * sigma * (1.0 + gate * (1.0 - sigma))).astype(BF16)
        up_delta = (back * gate * sigma).astype(BF16)
        mine = gather(jnp.stack([hidden, gate_delta, up_delta])).reshape(3, half, size)
        state = backward(mine, swap(mine), xt, gt, weights, rights, start, size, state)
    acc, low, gate_grad, up_grad, down_grad = state
    low = low.astype(BF16)
    mixed = acc[0]
    grad = acc[1]
    mixed = mixed + dot(low[0], lefts[2], NT)
    grad = grad + dot(low[1], lefts[0], NT) + dot(low[2], lefts[1], NT)
    out = [
        lax.psum_scatter(
            ordered(v, 0), "col", scatter_dimension=0, tiled=True
        ).astype(BF16)
        for v in (mixed, grad)
    ]
    return (out[0], out[1], gate_grad, up_grad, down_grad)


def solution(mesh):
    spec = P("row", "col")
    in_specs = (P(None, "row"),) * 2 + (spec,) * 9
    out_specs = (P("col", "row"),) * 2 + (spec,) * 3
    body = functools.partial(shards, mesh.shape["row"])
    return jax.shard_map(
        body, mesh=mesh, in_specs=in_specs, out_specs=out_specs, check_vma=False
    )
```
